32 devices in a mesh: dp: 8 (over z, x), expert: 4 (over y, core).
Axes of the slice: x: 2, y: 2, z: 4, core: 2. Of those that a mesh axis runs over, the one named last changes fastest.
Arguments:
- layer_input: bfloat16 [8192, 768], P(('dp', 'expert')), may hold values from -6 to 6
- output_grad: bfloat16 [8192, 768], P(('dp', 'expert')), may hold values from -6 to 6
- prev_logits: bfloat16 [8192, 12], P(('dp', 'expert')), may hold values from -3 to 3
- deal_order: int32 [8, 1024], P('dp', 'expert'), may hold values from 0 to 1023, each once within a row
- routes: int32 [8192, 2], P(('dp', 'expert')), may hold values from 0 to 11, all different within a row; in each aligned block of 256 rows (0 to 255, 256 to 511, ...) at most 64 rows name the same one
- lengths: int32 [32], P(('dp', 'expert')), may hold values from 1 to 256, 6144 in all
- attention_gain: float32 [768], replicated, may hold values from 0.1 to 1.9
- mixture_gain: float32 [768], replicated, may hold values from 0.1 to 1.9
- attention_in: bfloat16 [768, 2304], replicated, may hold values from -0.21875 to 0.21875
- attention_out: bfloat16 [768, 768], replicated, may hold values from -1.75 to 1.75
- router_weight: bfloat16 [768, 12], replicated, may hold values from -0.15625 to 0.15625
- constant_mix: bfloat16 [768, 4], replicated, may hold values from -0.15625 to 0.15625
- constant_value: bfloat16 [768, 2], replicated, may hold values from -4 to 4
- expert_gate_up: bfloat16 [8, 768, 4096], P('expert'), may hold values from -0.21875 to 0.21875
- expert_down: bfloat16 [8, 2048, 768], P('expert'), may hold values from -0.25 to 0.25
Outputs:
- layer_output: bfloat16 [8192, 768], P(('dp', 'expert'))
- input_grad: bfloat16 [8192, 768], P(('dp', 'expert'))
- prev_grad: bfloat16 [8192, 12], P(('dp', 'expert'))
- attention_gain_grad: float32 [768], P('dp')
- mixture_gain_grad: float32 [768], P('dp')
- attention_in_grad: float32 [768, 2304], P('dp')
- attention_out_grad: float32 [768, 768], P('dp')
- router_grad: float32 [768, 12], P('dp')
- constant_mix_grad: float32 [768, 4], P('dp')
- constant_value_grad: float32 [768, 2], P('dp')
- gate_up_grad: float32 [8, 768, 4096], P('expert', 'dp')
- down_grad: float32 [8, 2048, 768], P('expert', 'dp')
The draws below stay inside these ranges and needn't reach their ends.
Inputs may be any that keep to these rules, and one draw needn't show every extreme that they name: `routes`: each token names two different choices; among the rows of one device no choice is named by more than 64 rows, a bound that some block reaches. `deal_order`: each row is a permutation of 0 to 1023. `lengths`: they sum to 6144 and the longest is 256.
All inputs are finite; a program needn't handle non-finite values. No bound on the sum of `lengths` on one device may be relied on, other than what follows from the above.
Results may differ from the reference program's by a relative error of at most 0.017.
Values may be sent and summed in bfloat16 or wider, within the bound.
No kernel may reach another device: no remote copies, remote signals or barrier semaphores. Data moves between devices by JAX's collectives and lax.ppermute only.
A program may use at most 192 MiB of HBM per device.

```python
import math
import jax
import jax.numpy as jnp
import numpy as np
from jax import lax

D = 768
HEADS = 12
HDIM = 64
HID = 2048
EXPERTS = 8
TOPK = 2
TOK_DEV = 256
CAP = 64
CHOICES = 12
SLOTS = 32
GROUP_TOK = 1024
TOKENS = 8192
N_DP = 8


def block_levels(stream_key, shape, cuts, smallest, top_value):
    level = 1.0
    for axis_at, blocks in cuts:
        steps = jax.random.uniform(jax.random.fold_in(jax.random.fold_in(stream_key, 6), axis_at), (blocks,), jnp.float32, smallest / len(cuts), top_value / len(cuts))
        level = level * jnp.repeat(jnp.exp(steps), shape[axis_at] // blocks).reshape((-1,) + (1,) * (len(shape) - 1 - axis_at))
    return level


def profile(count, total, bound, skew):
    weights = [(1 << 20) // math.isqrt(grade ** skew) + 1 for grade in range(2, count + 1)]
    spare, given = total - bound - (count - 1), [1] * (count - 1)
    while spare > 0:
        candidates = [i for i in range(count - 1) if given[i] < bound]
        mass, budget = sum([weights[i] for i in candidates]), spare
        for i in candidates:
            more = min(bound - given[i], max(1, budget * weights[i] // mass), spare)
            given[i] = given[i] + more
            spare = spare - more
    return np.array([bound] + given)


def ragged(own_key, number_of, total, bound, slope):
    if number_of == 2:
        one = jax.random.randint(own_key, (), max(1, total - bound), min(bound, total - 1) + 1)
        return jnp.stack([one, total - one])
    tallies = jnp.asarray(profile(number_of, total, bound, slope), jnp.int32)
    pairs = (number_of - 1) // 2
    donor, taker = tallies[1:1 + 2 * pairs:2], tallies[2:2 + 2 * pairs:2]
    margin = jnp.minimum(donor - 1, bound - taker)
    moved = jax.random.randint(jax.random.fold_in(own_key, 1), (pairs,), 0, 1 << 20) % (margin + 1)
    tallies = tallies.at[1:1 + 2 * pairs:2].set(donor - moved).at[2:2 + 2 * pairs:2].set(taker + moved)
    return tallies[jax.random.permutation(jax.random.fold_in(own_key, 2), number_of)]


def routed_block(stream_key, own, number, rows, number_of, top, reach, slope):
    order = jax.random.permutation(stream_key, number_of)
    crowded, common = portions_of(number_of, rows * top, reach, slope, True), portions_of(number_of, rows * top, reach, slope, False)
    places = jnp.arange(number_of)

    def named(sizes, offset_by):
        used = int((sizes > 0).sum())
        fixed = max(1, used // 4)
        passed = fixed + (places - fixed + offset_by * (used - fixed)) % max(1, number_of - fixed)
        return jnp.zeros((number_of,), jnp.int32).at[order[jnp.where(places < fixed, places, passed)]].set(jnp.asarray(sizes, jnp.int32))

    sizes = jnp.where(number % 4 == 0, named(crowded, number // 4), named(common, number - number // 4 - 1))
    mixed = jax.random.permutation(jax.random.fold_in(own, 3), number_of)
    donor, sink = mixed[0:number_of // 2 * 2:2], mixed[1:number_of // 2 * 2:2]
    room = jnp.minimum(sizes[donor] - 1, reach - sizes[sink]) // 2
    room = jnp.where((donor == order[0]) | (sink == order[0]) | (sizes[sink] == 0), 0, jnp.maximum(room, 0))
    passed = jax.random.randint(jax.random.fold_in(own, 4), (number_of // 2,), 0, 1 << 20) % (room + 1)
    sizes = sizes.at[donor].add(-passed).at[sink].add(passed)
    items = jnp.searchsorted(jnp.cumsum(sizes), jnp.arange(rows * top), side="right").astype(jnp.int32)
    grid = items.reshape(top, rows).T
    grid = grid[jax.random.permutation(jax.random.fold_in(own, 1), rows)]
    offset_by = jax.random.randint(jax.random.fold_in(own, 2), (rows, 1), 0, top)
    return jnp.take_along_axis(grid, (jnp.arange(top)[None, :] + offset_by) % top, axis=1)


def portions_of(count, total, limit, slope, full):
    loads = [(1 << 20) // math.isqrt(standing ** slope) + 1 for standing in range(1, count + 1)]
    largest = limit if full else min(limit, max(-(-total // count), total * loads[0] // sum(loads)))
    least = 1 if total - largest >= count - 1 else 0
    counts, rest = [largest] + [least] * (count - 1), total - largest - least * (count - 1)
    while rest > 0:
        movable = [i for i in range(1, count) if counts[i] < largest] or [i for i in range(1, count) if counts[i] < limit]
        pool, budget = sum([loads[i] for i in movable]), rest
        for i in movable:
            more = min(limit - counts[i], max(1, budget * loads[i] // pool), rest)
            counts[i] = counts[i] + more
            rest = rest - more
    return np.array(counts)


def noise(rng, shape, spread, most, split=(), held_as=jnp.bfloat16):
    drawn = jax.random.normal(rng, shape, jnp.float32) * spread
    if len(split) > 0:
        drawn = block_levels(rng, shape, split, -0.22, 0.18) * drawn
    return jnp.clip(drawn, min=-most, max=most).astype(held_as)


def setup_inputs(seed: int = 0) -> dict:
    splits = jax.random.split(jax.random.key(seed), 16)
    layer_input = noise(splits[0], (TOKENS, D), 1.0, 6.0, ((0, 32),))
    output_grad = noise(splits[1], (TOKENS, D), 1.0, 6.0, ((0, 32),))
    prev_logits = noise(splits[2], (TOKENS, CHOICES), 0.5, 3.0, ((0, 32),))
    deal_order = jax.vmap(lambda own: jax.random.permutation(own, GROUP_TOK))(jax.random.split(splits[3], N_DP)).reshape((N_DP, GROUP_TOK)).astype(jnp.int32)
    routes_keys = jax.random.split(jax.random.fold_in(splits[4], 1), TOKENS // TOK_DEV)
    routes_turns = jax.random.permutation(jax.random.fold_in(splits[4], 3), TOKENS // TOK_DEV)
    routes = jax.vmap(lambda own, number: routed_block(jax.random.fold_in(splits[4], 2), own, number, TOK_DEV, CHOICES, TOPK, CAP, 1))(routes_keys, routes_turns).reshape((TOKENS, TOPK))
    lengths = ragged(splits[5], SLOTS, SLOTS * TOK_DEV * 3 // 4, TOK_DEV, 1).astype(jnp.int32)
    attention_gain = jnp.clip(1.0 + 0.18 * jax.random.normal(splits[6], (D,), jnp.float32), 0.1, 1.9)
    mixture_gain = jnp.clip(1.0 + 0.18 * jax.random.normal(splits[7], (D,), jnp.float32), 0.1, 1.9)
    attention_in = noise(splits[8], (D, 3 * D), D ** -0.5, 0.21875)
    attention_out = noise(splits[9], (D, D), (max(D // 64, 1)) ** -0.5, 1.75)
    router_weight = noise(splits[10], (D, CHOICES), (2 * D) ** -0.5, 0.15625)
    constant_mix = noise(splits[11], (D, 4), (2 * D) ** -0.5, 0.15625)
    constant_value = noise(splits[12], (D, 2), 1.0, 4.0)
    expert_gate_up = noise(splits[13], (EXPERTS, D, 2 * HID), D ** -0.5, 0.21875, ((0, 4),))
    expert_down = noise(splits[14], (EXPERTS, HID, D), (HID // 4) ** -0.5, 0.25, ((0, 4),))
    return {"layer_input": layer_input, "output_grad": output_grad, "prev_logits": prev_logits, "deal_order": deal_order, "routes": routes, "lengths": lengths, "attention_gain": attention_gain, "mixture_gain": mixture_gain, "attention_in": attention_in, "attention_out": attention_out, "router_weight": router_weight, "constant_mix": constant_mix, "constant_value": constant_value, "expert_gate_up": expert_gate_up, "expert_down": expert_down}


@jax.custom_vjp
def low(v):
    return lax.optimization_barrier(v.astype(jnp.bfloat16)).astype(jnp.float32)

@jax.custom_vjp
def low_back(v):
    return v

def low_keep(v):
    return (low(v), None)

def low_pass(kept, grad):
    return (grad,)

def back_keep(v):
    return (v, None)

def back_low(kept, grad):
    return (low(grad),)
low.defvjp(low_keep, low_pass)
low_back.defvjp(back_keep, back_low)
epsilon = 1e-06
rope_base = 10000.0
highest = lax.Precision.HIGHEST

def rms_norm(values, norm_gain):
    inverse = lax.rsqrt(lax.optimization_barrier(jnp.mean(values * values, axis=-1, keepdims=True)) + epsilon)
    return values * inverse * norm_gain

def rotate_pairs(values, cosine_table, sine_table):
    half_size = values.shape[-1] // 2
    first_half = values[..., :half_size]
    second_half = values[..., half_size:]
    return jnp.concatenate([first_half * cosine_table - second_half * sine_table, second_half * cosine_table + first_half * sine_table], axis=-1)

def group_layer(params, x_group, prev_group, order_group, routes_group, length_group):
    attention_gain, mixture_gain, attention_in, attention_out, router_weight, constant_mix, constant_value, expert_gate_up, expert_down = params
    dealt_rows = x_group[order_group]
    prev_dealt = prev_group[order_group]
    slot_count = length_group.shape[0]
    seq_len = TOK_DEV
    model_width = dealt_rows.shape[1]
    group_rows = dealt_rows.shape[0]
    normed_first = low(rms_norm(dealt_rows, attention_gain))
    projected = low_back(jnp.dot(normed_first, attention_in, precision=highest))
    projected = projected.reshape(slot_count, seq_len, 3, HEADS, HDIM)
    half_size = HDIM // 2
    positions = jnp.arange(seq_len, dtype=jnp.float32)
    inverse_freq = rope_base ** (-jnp.arange(half_size, dtype=jnp.float32) / half_size)
    angles = positions[:, None] * inverse_freq[None, :]
    cosine_table = jnp.cos(angles)[:, None, :]
    sine_table = jnp.sin(angles)[:, None, :]
    query_rot = low(rotate_pairs(projected[:, :, 0], cosine_table, sine_table))
    key_rot = low(rotate_pairs(projected[:, :, 1], cosine_table, sine_table))
    value_low = low(projected[:, :, 2])
    scores = low_back(jnp.einsum('sihd,sjhd->shij', query_rot, key_rot, precision=highest) * HDIM ** (-0.5))
    index_pos = jnp.arange(seq_len, dtype=jnp.int32)
    causal = index_pos[None, :] <= index_pos[:, None]
    allowed = causal[None, None] & (index_pos[None, None, None, :] < length_group[:, None, None, None])
    scores = jnp.where(allowed, scores, -jnp.inf)
    score_probs = low(jax.nn.softmax(scores, axis=-1))
    attended = low_back(low(jnp.einsum('shij,sjhd->sihd', score_probs, value_low, precision=highest)))
    attended = attended.reshape(group_rows, model_width)
    residual = dealt_rows + low_back(jnp.dot(attended, attention_out, precision=highest))
    normed_second = rms_norm(residual, mixture_gain)
    second_low = low(normed_second)
    logits = jnp.dot(second_low, router_weight, precision=highest) + prev_dealt
    picked = jnp.take_along_axis(logits, routes_group, axis=1)
    gate_values = jax.nn.softmax(picked, axis=-1)
    mix_logits = jnp.dot(second_low, constant_mix, precision=highest).reshape(group_rows, 2, 2)
    mix_weights = jax.nn.softmax(mix_logits, axis=-1)
    const_out = mix_weights[:, :, 0:1] * normed_second[:, None, :] + mix_weights[:, :, 1:2] * constant_value.T[None]
    flat_routes = routes_group.reshape(slot_count, seq_len * TOPK)
    route_onehot = (flat_routes[..., None] == jnp.arange(CHOICES, dtype=jnp.int32)).astype(jnp.int32)
    route_rank = lax.optimization_barrier(jnp.sum((jnp.cumsum(route_onehot, axis=1) - 1) * route_onehot, axis=2)).astype(jnp.int32)
    is_ffn = flat_routes < EXPERTS
    target = jnp.where(is_ffn, flat_routes * CAP + route_rank, EXPERTS * CAP).astype(jnp.int32)
    slot_ids = jnp.arange(slot_count, dtype=jnp.int32)
    row_ids = (jnp.arange(seq_len * TOPK, dtype=jnp.int32) // TOPK)[None, :] + slot_ids[:, None] * seq_len
    table = jnp.full((slot_count, EXPERTS * CAP + 1), group_rows, jnp.int32)
    table = table.at[slot_ids[:, None], target].set(row_ids.astype(jnp.int32))
    table = table[:, :EXPERTS * CAP].reshape(slot_count, EXPERTS, CAP).transpose(1, 0, 2).reshape(EXPERTS, slot_count * CAP)
    padded_input = jnp.concatenate([second_low, jnp.zeros((1, model_width), second_low.dtype)], axis=0)
    expert_rows = low_back(padded_input[table])
    gate_up = low_back(jnp.einsum('erd,edf->erf', expert_rows, expert_gate_up, precision=highest))
    inner_low = low(jax.nn.silu(gate_up[..., :HID]) * gate_up[..., HID:])
    expert_out = low_back(low(jnp.einsum('erf,efd->erd', inner_low, expert_down, precision=highest)))
    flat_out = expert_out.reshape(EXPERTS * slot_count * CAP, model_width)
    where_out = jnp.where(is_ffn, flat_routes * (slot_count * CAP) + slot_ids[:, None] * CAP + route_rank, 0).astype(jnp.int32)
    route_out = flat_out[where_out.reshape(group_rows, TOPK)]
    ffn_mask = (routes_group < EXPERTS)[..., None]
    copy_mask = (routes_group == EXPERTS + 1)[..., None]
    first_const = (routes_group == EXPERTS + 2)[..., None]
    second_const = (routes_group == EXPERTS + 3)[..., None]
    branch = jnp.where(ffn_mask, route_out, 0.0) + jnp.where(copy_mask, normed_second[:, None, :], 0.0) + jnp.where(first_const, const_out[:, 0][:, None, :], 0.0) + jnp.where(second_const, const_out[:, 1][:, None, :], 0.0)
    output = residual + lax.optimization_barrier(jnp.sum(gate_values[..., None] * branch, axis=1))
    return jnp.zeros_like(output).at[order_group].set(output)

def reference(layer_input, output_grad, prev_logits, deal_order, routes, lengths, attention_gain, mixture_gain, attention_in, attention_out, router_weight, constant_mix, constant_value, expert_gate_up, expert_down):
    params = tuple((item.astype(jnp.float32) for item in (attention_gain, mixture_gain, attention_in, attention_out, router_weight, constant_mix, constant_value, expert_gate_up, expert_down)))
    groups = deal_order.shape[0]
    x_all = layer_input.astype(jnp.float32).reshape(groups, -1, D)
    prev_all = prev_logits.astype(jnp.float32).reshape(groups, -1, CHOICES)
    route_all = routes.reshape(groups, -1, TOPK)
    length_all = lengths.reshape(groups, -1)

    def forward(params, x_all, prev_all):
        layer = jax.checkpoint(group_layer)

        def step(carry, item):
            x_group, prev_group, order_group, routes_group, length_group = item
            return (carry, layer(params, x_group, prev_group, order_group, routes_group, length_group))
        _, result = lax.scan(step, jnp.zeros((), jnp.float32), (x_all, prev_all, deal_order, route_all, length_all))
        return result
    output, pullback = jax.vjp(forward, params, x_all, prev_all)
    param_grads, input_grads, prev_grads = pullback(output_grad.astype(jnp.float32).reshape(groups, -1, D))
    return (output.reshape(-1, D).astype(jnp.bfloat16), input_grads.reshape(-1, D).astype(jnp.bfloat16), prev_grads.reshape(-1, CHOICES).astype(jnp.bfloat16), param_grads[0], param_grads[1], param_grads[2], param_grads[3], param_grads[4], param_grads[5], param_grads[6], param_grads[7], param_grads[8])
```

```python
import jax
import jax.numpy as jnp
from jax import lax
from jax.sharding import PartitionSpec as P

HEADS = 12

epsilon = 1e-06
rope_base = 10000.0
highest = lax.Precision.HIGHEST
low = jnp.bfloat16
wide = jnp.float32


def mm(left, right):
    return jnp.dot(left, right, preferred_element_type=wide)


def mm_tn(left, right):
    return lax.dot_general(left, right, (((0,), (0,)), ((), ())), preferred_element_type=wide)


def norm_forward(values, norm_gain):
    inverse = lax.rsqrt(jnp.mean(values * values, axis=-1, keepdims=True) + epsilon)
    unit_rows = values * inverse
    return (unit_rows * norm_gain, unit_rows, inverse)


def norm_backward(upstream, unit_rows, inverse, norm_gain):
    scaled = upstream * norm_gain
    gain_grad = jnp.sum(upstream * unit_rows, axis=0)
    back_rows = inverse * (
        scaled - unit_rows * jnp.mean(scaled * unit_rows, axis=-1, keepdims=True)
    )
    return (back_rows, gain_grad)


def rope_tables(count, half_size):
    positions = jnp.arange(count, dtype=jnp.float32)
    inverse_freq = rope_base ** (-jnp.arange(half_size, dtype=jnp.float32) / half_size)
    angles = positions[:, None] * inverse_freq[None, :]
    return (jnp.cos(angles)[:, None, :], jnp.sin(angles)[:, None, :])


def rotate(values, cosine_table, sine_table, sign):
    half_size = values.shape[-1] // 2
    first_half = values[..., :half_size]
    second_half = values[..., half_size:]
    return jnp.concatenate(
        [
            first_half * cosine_table - sign * second_half * sine_table,
            second_half * cosine_table + sign * first_half * sine_table,
        ],
        axis=-1,
    )


class Plan:
    def __init__(self):
        self.dp = lax.axis_size("dp")
        self.peers = lax.axis_size("expert")
        self.near = self.dp == 8 and self.peers == 4
        self.me = lax.axis_index("expert")
        self.row = lax.axis_index("dp")

    def flip(self, value, mask):
        return lax.ppermute(value, "expert", [(i, i ^ mask) for i in range(4)])

    def across(self, value):
        return lax.ppermute(value, "dp", [(i, i ^ 1) for i in range(8)])

    def along(self, value, step, begin, end):
        pairs = [(z * 2 + x, (z + step) * 2 + x) for z in range(begin, end) for x in range(2)]
        return lax.ppermute(value, "dp", pairs)

    def peer_order(self):
        if self.near:
            return self.me ^ jnp.array([0, 2, 1, 3], jnp.int32)
        return jnp.arange(self.peers, dtype=jnp.int32)

    def gather_peers(self, value):
        if not self.near:
            return lax.all_gather(value, "expert", axis=0)
        pair = jnp.stack([value, self.flip(value, 2)])
        return jnp.concatenate([pair, self.flip(pair, 1)], axis=0)

    def group_order(self):
        if self.near:
            z, x = self.row // 2, self.row % 2
            same = [((z - j) % 4) * 2 + x for j in range(4)]
            other = [((z - j) % 4) * 2 + 1 - x for j in range(4)]
            return jnp.stack(same + other)
        return jnp.arange(self.dp, dtype=jnp.int32)

    def gather_groups(self, value):
        if not self.near:
            every = lax.all_gather(value, "dp", axis=0)
            return [every[i] for i in range(self.dp)]
        right_1 = self.along(value, 1, 0, 3)
        left_1 = self.along(value, -1, 1, 4)
        right_2 = self.along(right_1, 1, 1, 3)
        left_2 = self.along(left_1, -1, 1, 3)
        right_3 = self.along(right_2, 1, 2, 3)
        left_3 = self.along(left_2, -1, 1, 2)
        same = [value, right_1 + left_3, right_2 + left_2, right_3 + left_1]
        return same + [self.across(block) for block in same]

    def swap_groups(self, value):
        if not self.near:
            return lax.all_to_all(value, "dp", 0, 0, tiled=True)
        parts = []
        for mask in range(8):
            part = lax.dynamic_index_in_dim(value, self.row ^ mask, 0, keepdims=False)
            if mask:
                part = lax.ppermute(part, "dp", [(i, i ^ mask) for i in range(8)])
            parts.append(part)
        return jnp.take(jnp.stack(parts), self.row ^ jnp.arange(8), axis=0)

    def sum_rows(self, partial):
        if not self.near:
            total = lax.psum(partial.astype(low).astype(wide), "expert")
            return lax.psum_scatter(total, "dp", scatter_dimension=0, tiled=True)[0]
        width = partial.shape[-1] // 4
        core, high = self.me % 2, self.me // 2
        z, x = self.row // 2, self.row % 2
        take = lax.dynamic_slice_in_dim
        keep = take(partial, core * 2 * width, 2 * width, 2)
        send = take(partial, (1 - core) * 2 * width, 2 * width, 2).astype(low)
        keep = keep + self.flip(send, 1).astype(wide)
        send = take(keep, (1 - high) * width, width, 2).astype(low)
        keep = take(keep, high * width, width, 2)
        keep = keep + self.flip(send, 2).astype(wide)
        keep = keep.reshape(4, 2, *keep.shape[1:])
        send = lax.dynamic_index_in_dim(keep, 1 - x, 1, keepdims=False).astype(low)
        keep = lax.dynamic_index_in_dim(keep, x, 1, keepdims=False)
        keep = keep + self.across(send).astype(wide)
        total = lax.dynamic_index_in_dim(keep, z, 0, keepdims=False)
        sent = keep.astype(low)
        for step in (1, 2, 3):
            part = lax.dynamic_index_in_dim(sent, (z + step) % 4, 0, keepdims=False)
            pairs = [(a * 2 + b, ((a + step) % 4) * 2 + b) for a in range(4) for b in range(2)]
            total = total + lax.ppermute(part, "dp", pairs).astype(wide)
        mine = total.astype(low)
        parts = jnp.stack([mine] + [self.flip(mine, mask) for mask in (1, 2, 3)])
        columns = jnp.take(parts, self.me ^ jnp.array([0, 2, 1, 3], jnp.int32), axis=0)
        return jnp.concatenate([columns[i] for i in range(4)], axis=-1).astype(wide)


def local(
    layer_input,
    output_grad,
    prev_logits,
    deal_order,
    routes,
    lengths,
    attention_gain,
    mixture_gain,
    attention_in,
    attention_out,
    router_weight,
    constant_mix,
    constant_value,
    expert_gate_up,
    expert_down,
):
    plan = Plan()
    tok_count = layer_input.shape[0]
    model_width = layer_input.shape[1]
    choice_count = prev_logits.shape[1]
    local_experts = expert_gate_up.shape[0]
    hidden_units = expert_down.shape[1]
    peer_count = plan.peers
    experts_all = local_experts * peer_count
    capacity = tok_count // 4
    send_rows = experts_all * capacity
    head_count = HEADS
    head_size = model_width // head_count
    half_size = head_size // 2
    score_scale = head_size ** (-0.5)
    slot_order = deal_order[0]
    iota = jnp.arange(tok_count, dtype=jnp.int32)

    group_x = plan.gather_peers(layer_input).reshape(-1, model_width)
    group_dy = plan.gather_peers(output_grad).reshape(-1, model_width)
    group_prev = plan.gather_peers(prev_logits).reshape(-1, choice_count)
    group_slots = plan.gather_peers(deal_order).reshape(-1)
    given_rows = (plan.peer_order()[:, None] * tok_count + iota[None, :]).reshape(-1)
    deal_pick = (slot_order[:, None] == given_rows[None, :]).astype(low)
    own_rows = plan.me * tok_count + iota
    home_pick = (group_slots[None, :] == own_rows[:, None]).astype(low)

    dealt_rows = mm(deal_pick, group_x)
    dy_low = mm(deal_pick, group_dy).astype(low)
    prev_dealt = mm(deal_pick, group_prev)
    grad_out = dy_low.astype(wide)

    choices = jnp.arange(choice_count, dtype=jnp.int32)
    route_onehot = (routes[..., None] == choices).astype(wide)
    hits = jnp.sum(route_onehot, axis=1)
    earlier = mm((iota[None, :] < iota[:, None]).astype(low), hits.astype(low))
    rank = jnp.sum(route_onehot * earlier[:, None, :], axis=-1).astype(jnp.int32)
    is_ffn = routes < experts_all
    target = jnp.where(is_ffn, routes * capacity + rank, send_rows)
    places = jnp.arange(send_rows, dtype=jnp.int32)
    pick_0 = target[:, 0][:, None] == places[None, :]
    pick_1 = target[:, 1][:, None] == places[None, :]
    both_pick = (pick_0 | pick_1).astype(low)

    def to_experts(rows):
        outgoing = mm_tn(both_pick, rows).astype(low)
        outgoing = outgoing.reshape(peer_count, local_experts * capacity, model_width)
        incoming = lax.all_to_all(outgoing, "expert", split_axis=0, concat_axis=0, tiled=True)
        incoming = incoming.reshape(peer_count, local_experts, capacity, model_width)
        return incoming.transpose(1, 0, 2, 3).reshape(local_experts, -1, model_width)

    def from_experts(rows):
        rows = rows.reshape(local_experts, peer_count, capacity, model_width).transpose(1, 0, 2, 3)
        rows = rows.reshape(peer_count, local_experts * capacity, model_width)
        rows = lax.all_to_all(rows, "expert", split_axis=0, concat_axis=0, tiled=True)
        return rows.reshape(send_rows, model_width)

    dy_in = to_experts(dy_low)
    dy_blocks = plan.gather_groups(dy_in)

    normed_first, unit_first, inverse_first = norm_forward(dealt_rows, attention_gain)
    first_low = normed_first.astype(low)
    projected = mm(first_low, attention_in)
    projected = projected.reshape(tok_count, 3, head_count, head_size)
    cosine_table, sine_table = rope_tables(tok_count, half_size)
    query_rot = rotate(projected[:, 0], cosine_table, sine_table, 1.0).astype(low)
    key_rot = rotate(projected[:, 1], cosine_table, sine_table, 1.0).astype(low)
    value_low = projected[:, 2].astype(low)
    allowed = (iota[None, :] <= iota[:, None]) & (iota[None, :] < lengths[0])
    raw_scores = (
        jnp.einsum("ihd,jhd->hij", query_rot, key_rot, preferred_element_type=wide) * score_scale
    )
    scores = jnp.where(allowed[None], raw_scores, -jnp.inf)
    score_peak = jnp.max(scores, axis=-1, keepdims=True)
    exp_scores = jnp.exp(scores - score_peak)
    score_probs = exp_scores / jnp.sum(exp_scores, axis=-1, keepdims=True)
    probs_low = score_probs.astype(low)
    attended = (
        jnp.einsum("hij,jhd->ihd", probs_low, value_low, preferred_element_type=wide)
        .astype(low)
        .reshape(tok_count, model_width)
    )
    residual = dealt_rows + mm(attended, attention_out)
    normed_second, unit_second, inverse_second = norm_forward(residual, mixture_gain)
    second_low = normed_second.astype(low)

    x_in = to_experts(second_low)
    x_blocks = plan.gather_groups(x_in)

    logits = mm(second_low, router_weight) + prev_dealt
    picked = jnp.sum(route_onehot * logits[:, None, :], axis=-1)
    gate_values = jax.nn.softmax(picked, axis=-1)
    gates_sent = jnp.sum(
        jnp.where(pick_0, gate_values[:, 0:1], 0.0) + jnp.where(pick_1, gate_values[:, 1:2], 0.0), axis=0
    )
    gates_all = lax.all_gather(gates_sent, ("dp", "expert"), axis=0)
    mix_logits = mm(second_low, constant_mix).reshape(tok_count, 2, 2)
    mix_weights = jax.nn.softmax(mix_logits, axis=-1)
    const_rows = constant_value.astype(wide).T
    const_out = (
        mix_weights[:, :, 0:1] * normed_second[:, None, :]
        + mix_weights[:, :, 1:2] * const_rows[None]
    )

    def expert_forward(rows, gate_up_weight):
        gate_up = jnp.einsum("erd,edf->erf", rows, gate_up_weight, preferred_element_type=wide)
        width = gate_up_weight.shape[-1] // 2
        return gate_up[..., :width], gate_up[..., width:]

    def expert_back(gate_part, up_part, dy_rows, down_weight):
        sigmoid_gate = jax.nn.sigmoid(gate_part)
        grad_inner = jnp.einsum("erd,efd->erf", dy_rows, down_weight, preferred_element_type=wide)
        gate_back = grad_inner * up_part * sigmoid_gate * (1.0 + gate_part * (1.0 - sigmoid_gate))
        return jnp.concatenate([gate_back, grad_inner * gate_part * sigmoid_gate], axis=-1)

    gate_part, up_part = expert_forward(x_in, expert_gate_up)
    inner_low = (jax.nn.silu(gate_part) * up_part).astype(low)
    produced = jnp.einsum("erf,efd->erd", inner_low, expert_down, preferred_element_type=wide)
    returned = from_experts(produced.astype(low))
    back_gate_up = expert_back(gate_part, up_part, dy_in, expert_down).astype(low)
    row_grads = jnp.einsum("erf,edf->erd", back_gate_up, expert_gate_up, preferred_element_type=wide)
    row_grads = from_experts(row_grads.astype(low))

    pick_0_low, pick_1_low = pick_0.astype(low), pick_1.astype(low)
    route_out = jnp.stack([mm(pick_0_low, returned), mm(pick_1_low, returned)], axis=1)
    copy_mask = routes == experts_all + 1
    const_mask = routes[..., None] == (experts_all + 2 + jnp.arange(2, dtype=jnp.int32))
    branch = (
        route_out
        + jnp.where(copy_mask[..., None], normed_second[:, None, :], 0.0)
        + jnp.where(const_mask[..., 0:1], const_out[:, 0][:, None, :], 0.0)
        + jnp.where(const_mask[..., 1:2], const_out[:, 1][:, None, :], 0.0)
    )
    output = residual + jnp.sum(gate_values[..., None] * branch, axis=1)
    group_out = plan.gather_peers(output.astype(low)).reshape(-1, model_width)
    out_rows = mm(home_pick, group_out).astype(low)

    grad_gate = jnp.sum(branch * grad_out[:, None, :], axis=-1)
    grad_picked = gate_values * (
        grad_gate - jnp.sum(gate_values * grad_gate, axis=-1, keepdims=True)
    )
    grad_logits = jnp.sum(route_onehot * grad_picked[..., None], axis=1)
    expert_input_grad = gate_values[:, 0:1] * mm(pick_0_low, row_grads) + gate_values[
        :, 1:2
    ] * mm(pick_1_low, row_grads)
    const_weight = jnp.sum(jnp.where(const_mask, gate_values[..., None], 0.0), axis=1)
    copy_weight = jnp.sum(jnp.where(copy_mask, gate_values, 0.0), axis=1)
    along_normed = jnp.sum(grad_out * normed_second, axis=-1)
    along_value = mm(dy_low, constant_value)
    grad_mix = jnp.stack(
        [const_weight * along_normed[:, None], const_weight * along_value], axis=-1
    )
    grad_mixlog = mix_weights * (grad_mix - jnp.sum(mix_weights * grad_mix, axis=-1, keepdims=True))
    grad_mixlog = grad_mixlog.reshape(tok_count, 4)
    second_wide = second_low.astype(wide)
    narrow = jnp.concatenate([grad_logits, grad_mixlog], axis=1)
    narrow_grad = jnp.dot(second_wide.T, narrow, precision=highest)
    value_grad = jnp.dot(grad_out.T, const_weight * mix_weights[:, :, 1], precision=highest)
    direct_scale = copy_weight + jnp.sum(const_weight * mix_weights[:, :, 0], axis=1)
    narrow_weight = jnp.concatenate([router_weight, constant_mix], axis=1).astype(wide)
    grad_second = (
        direct_scale[:, None] * grad_out
        + expert_input_grad
        + jnp.dot(narrow, narrow_weight.T, precision=highest)
    )
    back_second, gain_second = norm_backward(grad_second, unit_second, inverse_second, mixture_gain)
    grad_residual = grad_out + back_second

    grad_attn = grad_residual.astype(low)
    out_partial = mm_tn(attended, grad_attn)
    grad_attended = lax.dot_general(
        grad_attn, attention_out, (((1,), (1,)), ((), ())), preferred_element_type=wide
    )
    grad_attended = grad_attended.astype(low).reshape(tok_count, head_count, head_size)
    grad_value = jnp.einsum("hij,ihd->jhd", probs_low, grad_attended, preferred_element_type=wide)
    grad_probs = jnp.einsum("ihd,jhd->hij", grad_attended, value_low, preferred_element_type=wide)
    grad_scores = (
        score_probs * (grad_probs - jnp.sum(score_probs * grad_probs, axis=-1, keepdims=True))
    ).astype(low)
    grad_query = (
        jnp.einsum("hij,jhd->ihd", grad_scores, key_rot, preferred_element_type=wide) * score_scale
    )
    grad_key = (
        jnp.einsum("hij,ihd->jhd", grad_scores, query_rot, preferred_element_type=wide)
        * score_scale
    )
    grad_qkv = jnp.stack(
        [
            rotate(grad_query, cosine_table, sine_table, -1.0),
            rotate(grad_key, cosine_table, sine_table, -1.0),
            grad_value,
        ],
        axis=1,
    )
    grad_qkv = grad_qkv.reshape(tok_count, 3 * model_width).astype(low)
    in_partial = mm_tn(first_low, grad_qkv)
    grad_first = lax.dot_general(
        grad_qkv, attention_in, (((1,), (1,)), ((), ())), preferred_element_type=wide
    )
    back_first, gain_first = norm_backward(grad_first, unit_first, inverse_first, attention_gain)
    grad_dealt = grad_residual + back_first

    group_back = plan.gather_peers(grad_dealt.astype(low)).reshape(-1, model_width)
    input_rows = mm(home_pick, group_back).astype(low)
    group_logits = plan.gather_peers(grad_logits.astype(low)).reshape(-1, choice_count)
    prev_rows = mm(home_pick, group_logits).astype(low)

    share_rows = model_width // plan.dp
    matrices = jnp.concatenate([in_partial, out_partial], axis=1).reshape(plan.dp, share_rows, -1)
    narrow_all = jnp.concatenate(
        [narrow_grad, value_grad, gain_first[:, None], gain_second[:, None]], axis=1
    )
    narrow_count = narrow_all.shape[1]
    flat = narrow_all.reshape(plan.dp, 1, share_rows * narrow_count)
    flat = jnp.pad(flat, ((0, 0), (0, 7), (0, 4 * model_width - share_rows * narrow_count)))
    total = plan.sum_rows(jnp.concatenate([matrices, flat], axis=1))
    in_grad = total[:share_rows, : 3 * model_width]
    out_grad = total[:share_rows, 3 * model_width :]
    narrow_sum = total[share_rows, : share_rows * narrow_count].reshape(share_rows, narrow_count)

    share = hidden_units // plan.dp
    first_unit = plan.row * share
    gate_weight = lax.dynamic_slice_in_dim(expert_gate_up, first_unit, share, 2)
    up_weight = lax.dynamic_slice_in_dim(expert_gate_up, hidden_units + first_unit, share, 2)
    down_weight = lax.dynamic_slice_in_dim(expert_down, first_unit, share, 1)
    x_all = jnp.concatenate(x_blocks, axis=1)
    dy_all = jnp.concatenate(dy_blocks, axis=1)
    gates_all = gates_all.reshape(plan.dp, peer_count, peer_count, local_experts, capacity)
    gates_all = lax.dynamic_index_in_dim(gates_all, plan.me, 2, keepdims=False)
    gates_all = jnp.take(gates_all, plan.group_order(), axis=0)
    gates_all = gates_all.transpose(2, 0, 1, 3).reshape(local_experts, -1)[..., None]
    gate_part, up_part = expert_forward(x_all, jnp.concatenate([gate_weight, up_weight], axis=-1))
    gated_inner = (jax.nn.silu(gate_part) * up_part * gates_all).astype(low)
    down_sum = jnp.einsum("erf,erd->efd", gated_inner, dy_all, preferred_element_type=wide)
    back_all = (expert_back(gate_part, up_part, dy_all, down_weight) * gates_all).astype(low)
    up_partial = jnp.einsum("erd,erf->edf", x_all, back_all, preferred_element_type=wide)
    up_partial = up_partial.astype(low).reshape(local_experts, plan.dp, share_rows, 2 * share)
    swapped = plan.swap_groups(up_partial.transpose(1, 0, 2, 3))
    swapped = swapped.reshape(plan.dp, local_experts, share_rows, 2, share)
    gate_up_sum = swapped.transpose(1, 2, 3, 0, 4).reshape(local_experts, share_rows, -1)
    return (
        out_rows,
        input_rows,
        prev_rows,
        narrow_sum[:, choice_count + 6],
        narrow_sum[:, choice_count + 7],
        in_grad,
        out_grad,
        narrow_sum[:, :choice_count],
        narrow_sum[:, choice_count : choice_count + 4],
        narrow_sum[:, choice_count + 4 : choice_count + 6],
        gate_up_sum.astype(wide),
        down_sum,
    )


def solution(mesh):
    in_specs = (
        P(("dp", "expert"), None),
        P(("dp", "expert"), None),
        P(("dp", "expert"), None),
        P("dp", "expert"),
        P(("dp", "expert"), None),
        P(("dp", "expert")),
        P(),
        P(),
        P(),
        P(),
        P(),
        P(),
        P(),
        P("expert", None, None),
        P("expert", None, None),
    )
    out_specs = (
        P(("dp", "expert"), None),
        P(("dp", "expert"), None),
        P(("dp", "expert"), None),
        P("dp"),
        P("dp"),
        P("dp", None),
        P("dp", None),
        P("dp", None),
        P("dp", None),
        P("dp", None),
        P("expert", "dp", None),
        P("expert", "dp", None),
    )
    return jax.shard_map(local, mesh=mesh, in_specs=in_specs, out_specs=out_specs, check_vma=False)
```

```python
import functools

import jax
import jax.numpy as jnp
from jax import lax
from jax.experimental import pallas as pl
from jax.experimental.pallas import tpu as pltpu
from jax.sharding import PartitionSpec as P

HEADS = 12

epsilon = 1e-06
rope_base = 10000.0
highest = lax.Precision.HIGHEST
low = jnp.bfloat16
wide = jnp.float32


def mm(left, right):
    return jnp.dot(left, right, preferred_element_type=wide)


def mm_tn(left, right):
    return lax.dot_general(left, right, (((0,), (0,)), ((), ())), preferred_element_type=wide)


def mm_nt(left, right):
    return lax.dot_general(left, right, (((1,), (1,)), ((), ())), preferred_element_type=wide)


def norm_forward(values, norm_gain):
    inverse = lax.rsqrt(jnp.mean(values * values, axis=-1, keepdims=True) + epsilon)
    unit_rows = values * inverse
    return (unit_rows * norm_gain, unit_rows, inverse)


def norm_backward(upstream, unit_rows, inverse, norm_gain):
    scaled = upstream * norm_gain
    gain_grad = jnp.sum(upstream * unit_rows, axis=0)
    back_rows = inverse * (
        scaled - unit_rows * jnp.mean(scaled * unit_rows, axis=-1, keepdims=True)
    )
    return (back_rows, gain_grad)


def rope_tables(count, half_size):
    positions = jnp.arange(count, dtype=jnp.float32)
    inverse_freq = rope_base ** (-jnp.arange(half_size, dtype=jnp.float32) / half_size)
    angles = positions[:, None] * inverse_freq[None, :]
    return (jnp.cos(angles)[:, None, :], jnp.sin(angles)[:, None, :])


def rotate(values, cosine_table, sine_table, sign):
    half_size = values.shape[-1] // 2
    first_half = values[..., :half_size]
    second_half = values[..., half_size:]
    return jnp.concatenate(
        [
            first_half * cosine_table - sign * second_half * sine_table,
            second_half * cosine_table + sign * first_half * sine_table,
        ],
        axis=-1,
    )


class Plan:
    def __init__(self):
        self.dp = lax.axis_size("dp")
        self.peers = lax.axis_size("expert")
        self.near = self.dp == 8 and self.peers == 4
        self.me = lax.axis_index("expert")
        self.row = lax.axis_index("dp")

    def flip(self, value, mask):
        return lax.ppermute(value, "expert", [(i, i ^ mask) for i in range(4)])

    def across(self, value):
        return lax.ppermute(value, "dp", [(i, i ^ 1) for i in range(8)])

    def around(self, value, step):
        pairs = [(a * 2 + b, ((a + step) % 4) * 2 + b) for a in range(4) for b in range(2)]
        return lax.ppermute(value, "dp", pairs)

    def peer_order(self):
        if self.near:
            return self.me ^ jnp.array([0, 2, 1, 3], jnp.int32)
        return jnp.arange(self.peers, dtype=jnp.int32)

    def gather_peers(self, value):
        if not self.near:
            return lax.all_gather(value, "expert", axis=0)
        pair = jnp.stack([value, self.flip(value, 2)])
        return jnp.concatenate([pair, self.flip(pair, 1)], axis=0)

    def group_order(self):
        if self.near:
            z, x = self.row // 2, self.row % 2
            same = [((z - j) % 4) * 2 + x for j in range(4)]
            other = [((z - j) % 4) * 2 + 1 - x for j in range(4)]
            return jnp.stack(same + other)
        return jnp.arange(self.dp, dtype=jnp.int32)

    def gather_groups(self, value):
        if not self.near:
            every = lax.all_gather(value, "dp", axis=0)
            return [every[i] for i in range(self.dp)]
        same = [value] + [self.around(value, step) for step in (1, 2, 3)]
        return same + [self.across(block) for block in same]

    def swap_groups(self, value):
        if not self.near:
            return lax.all_to_all(value, "dp", 0, 0, tiled=True)
        parts = []
        for mask in range(8):
            part = lax.dynamic_index_in_dim(value, self.row ^ mask, 0, keepdims=False)
            if mask:
                part = lax.ppermute(part, "dp", [(i, i ^ mask) for i in range(8)])
            parts.append(part)
        return jnp.take(jnp.stack(parts), self.row ^ jnp.arange(8), axis=0)

    def sum_rows(self, partial):
        if not self.near:
            total = lax.psum(partial.astype(low).astype(wide), "expert")
            return lax.psum_scatter(total, "dp", scatter_dimension=0, tiled=True)[0]
        width = partial.shape[-1] // 4
        core, high = self.me % 2, self.me // 2
        z, x = self.row // 2, self.row % 2
        take = lax.dynamic_slice_in_dim
        keep = take(partial, core * 2 * width, 2 * width, 2)
        send = take(partial, (1 - core) * 2 * width, 2 * width, 2).astype(low)
        keep = keep + self.flip(send, 1).astype(wide)
        send = take(keep, (1 - high) * width, width, 2).astype(low)
        keep = take(keep, high * width, width, 2)
        keep = keep + self.flip(send, 2).astype(wide)
        keep = keep.reshape(4, 2, *keep.shape[1:])
        send = lax.dynamic_index_in_dim(keep, 1 - x, 1, keepdims=False).astype(low)
        keep = lax.dynamic_index_in_dim(keep, x, 1, keepdims=False)
        keep = keep + self.across(send).astype(wide)
        total = lax.dynamic_index_in_dim(keep, z, 0, keepdims=False)
        sent = keep.astype(low)
        for step in (1, 2, 3):
            part = lax.dynamic_index_in_dim(sent, (z + step) % 4, 0, keepdims=False)
            total = total + self.around(part, step).astype(wide)
        mine = total.astype(low)
        parts = jnp.stack([mine] + [self.flip(mine, mask) for mask in (1, 2, 3)])
        columns = jnp.take(parts, self.me ^ jnp.array([0, 2, 1, 3], jnp.int32), axis=0)
        return jnp.concatenate([columns[i] for i in range(4)], axis=-1).astype(wide)


def expert_parts(rows, dy_rows, gate_weight, up_weight, down_weight):
    gate_part = mm(rows, gate_weight)
    up_part = mm(rows, up_weight)
    sigmoid_gate = jax.nn.sigmoid(gate_part)
    silu_gate = gate_part * sigmoid_gate
    grad_inner = mm_nt(dy_rows, down_weight)
    gate_back = grad_inner * up_part * sigmoid_gate * (1.0 + gate_part * (1.0 - sigmoid_gate))
    return silu_gate * up_part, gate_back, grad_inner * silu_gate


def expert_body(x_ref, dy_ref, gate_ref, up_ref, down_ref, o_ref, out_sum, back_sum):
    step = pl.program_id(1)
    width = x_ref.shape[-1]
    rows = x_ref[...].reshape(-1, width)
    dy_rows = dy_ref[...].reshape(-1, width)
    inner, gate_back, up_back = expert_parts(rows, dy_rows, gate_ref[0], up_ref[0], down_ref[0])
    out_part = mm(inner.astype(low), down_ref[0])
    back_part = mm_nt(gate_back.astype(low), gate_ref[0]) + mm_nt(up_back.astype(low), up_ref[0])

    @pl.when(step == 0)
    def _():
        out_sum[...] = out_part
        back_sum[...] = back_part

    @pl.when(step > 0)
    def _():
        out_sum[...] += out_part
        back_sum[...] += back_part

    @pl.when(step == pl.num_programs(1) - 1)
    def _():
        peers, capacity = x_ref.shape[0], x_ref.shape[1]
        o_ref[:, 0] = out_sum[...].astype(low).reshape(peers, capacity, width)
        o_ref[:, 1] = back_sum[...].astype(low).reshape(peers, capacity, width)


def expert_call(x_in, dy_in, gate_up_weight, down_weight, capacity):
    peers, _, width = x_in.shape
    experts, hidden, _ = down_weight.shape
    tile = min(512, hidden)
    steps = hidden // tile
    rows = peers * capacity
    flops = 12 * experts * rows * width * hidden
    return pl.pallas_call(
        expert_body,
        grid=(experts, steps),
        in_specs=[
            pl.BlockSpec((peers, capacity, width), lambda e, j: (0, e, 0)),
            pl.BlockSpec((peers, capacity, width), lambda e, j: (0, e, 0)),
            pl.BlockSpec((1, width, tile), lambda e, j: (e, 0, j)),
            pl.BlockSpec((1, width, tile), lambda e, j: (e, 0, steps + j)),
            pl.BlockSpec((1, tile, width), lambda e, j: (e, j, 0)),
        ],
        out_specs=pl.BlockSpec((peers, 2, capacity, width), lambda e, j: (0, 0, e, 0)),
        out_shape=jax.ShapeDtypeStruct((peers, 2, experts * capacity, width), low),
        scratch_shapes=[pltpu.VMEM((rows, width), wide), pltpu.VMEM((rows, width), wide)],
        compiler_params=pltpu.CompilerParams(vmem_limit_bytes=40 << 20),
        cost_estimate=pl.CostEstimate(
            flops=flops, bytes_accessed=experts * hidden * width * 6, transcendentals=0
        ),
        name="experts",
    )(x_in, dy_in, gate_up_weight, gate_up_weight, down_weight)


def weights_body(groups, row_ref, *refs):
    x_refs, gate_rows = refs[:groups], refs[groups : 2 * groups]
    dy_refs = refs[2 * groups : 3 * groups]
    gate_ref, up_ref, down_ref, back_out, down_out, back_sum = refs[3 * groups :]
    expert = pl.program_id(0)
    peers, capacity, width = x_refs[0].shape
    share = gate_ref.shape[-1]
    lane = lax.broadcasted_iota(jnp.int32, (capacity, 128), 1)
    place = lax.broadcasted_iota(jnp.int32, (capacity, 128), 0) + expert * capacity
    for block in range(groups):
        rows = x_refs[block][...].reshape(-1, width)
        dy_rows = dy_refs[block][...].reshape(-1, width)
        columns = []
        for peer in range(peers):
            both = gate_rows[block][peer].astype(wide)
            both = both[0:1, 0:128] + both[0:1, 128:256]
            columns.append(jnp.sum(jnp.where(lane == place, both, 0.0), axis=1, keepdims=True))
        gates = jnp.concatenate(columns, axis=0)
        inner, gate_back, up_back = expert_parts(
            rows, dy_rows, gate_ref[0], up_ref[0], down_ref[0]
        )
        down_part = mm_tn((inner * gates).astype(low), dy_rows)
        gate_part = mm_tn(rows, (gate_back * gates).astype(low))
        up_part = mm_tn(rows, (up_back * gates).astype(low))
        if block == 0:
            down_out[0] = down_part
            back_sum[:, :share] = gate_part
            back_sum[:, share:] = up_part
        else:
            down_out[0] += down_part
            back_sum[:, :share] += gate_part
            back_sum[:, share:] += up_part
    back_out[0] = back_sum[...].astype(low)


def weights_call(x_blocks, dy_blocks, gate_up_weight, down_weight, row, capacity):
    groups = len(x_blocks)
    peers, _, width = x_blocks[0].shape
    experts, hidden, _ = down_weight.shape
    share = hidden // groups
    rows_spec = pl.BlockSpec((peers, capacity, width), lambda e, s: (0, e, 0))
    gate_row = experts * capacity // 8
    gates_spec = pl.BlockSpec((peers, 8, width), lambda e, s: (0, gate_row, 0))
    grid_spec = pltpu.PrefetchScalarGridSpec(
        num_scalar_prefetch=1,
        grid=(experts,),
        in_specs=[rows_spec] * groups
        + [gates_spec] * groups
        + [rows_spec] * groups
        + [
            pl.BlockSpec((1, width, share), lambda e, s: (e, 0, s[0])),
            pl.BlockSpec((1, width, share), lambda e, s: (e, 0, groups + s[0])),
            pl.BlockSpec((1, share, width), lambda e, s: (e, s[0], 0)),
        ],
        out_specs=[
            pl.BlockSpec((1, width, 2 * share), lambda e, s: (e, 0, 0)),
            pl.BlockSpec((1, share, width), lambda e, s: (e, 0, 0)),
        ],
        scratch_shapes=[pltpu.VMEM((width, 2 * share), wide)],
    )
    rows = groups * peers * capacity
    return pl.pallas_call(
        functools.partial(weights_body, groups),
        grid_spec=grid_spec,
        out_shape=[
            jax.ShapeDtypeStruct((experts, width, 2 * share), low),
            jax.ShapeDtypeStruct((experts, share, width), wide),
        ],
        compiler_params=pltpu.CompilerParams(vmem_limit_bytes=48 << 20),
        cost_estimate=pl.CostEstimate(
            flops=12 * experts * rows * width * share,
            bytes_accessed=4 * experts * rows * width,
            transcendentals=0,
        ),
        name="expert_weights",
    )(row, *x_blocks, *x_blocks, *dy_blocks, gate_up_weight, gate_up_weight, down_weight)


def weights_plain(x_blocks, dy_blocks, gate_up_weight, down_weight, row, capacity):
    peers, _, width = x_blocks[0].shape
    experts, hidden, _ = down_weight.shape
    share = hidden // len(x_blocks)
    first = row * share
    gate_weight = lax.dynamic_slice_in_dim(gate_up_weight, first, share, 2)
    up_weight = lax.dynamic_slice_in_dim(gate_up_weight, hidden + first, share, 2)
    down_weight = lax.dynamic_slice_in_dim(down_weight, first, share, 1)
    x_all, dy_all = jnp.stack(x_blocks), jnp.stack(dy_blocks)
    gate_lanes = x_all[:, :, experts * capacity].astype(wide)
    gate_lanes = gate_lanes[..., :128] + gate_lanes[..., 128:256]
    back, down = [], []
    for expert in range(experts):
        part = slice(expert * capacity, (expert + 1) * capacity)
        rows = x_all[:, :, part].reshape(-1, width)
        dy_rows = dy_all[:, :, part].reshape(-1, width)
        gates = gate_lanes[..., part].reshape(-1, 1)
        inner, gate_back, up_back = expert_parts(
            rows, dy_rows, gate_weight[expert], up_weight[expert], down_weight[expert]
        )
        back_rows = jnp.concatenate([gate_back, up_back], axis=1) * gates
        back.append(mm_tn(rows, back_rows.astype(low)).astype(low))
        down.append(mm_tn((inner * gates).astype(low), dy_rows))
    return jnp.stack(back), jnp.stack(down)


def local(
    layer_input,
    output_grad,
    prev_logits,
    deal_order,
    routes,
    lengths,
    attention_gain,
    mixture_gain,
    attention_in,
    attention_out,
    router_weight,
    constant_mix,
    constant_value,
    expert_gate_up,
    expert_down,
):
    plan = Plan()
    tok_count = layer_input.shape[0]
    model_width = layer_input.shape[1]
    choice_count = prev_logits.shape[1]
    local_experts = expert_gate_up.shape[0]
    hidden_units = expert_down.shape[1]
    peer_count = plan.peers
    experts_all = local_experts * peer_count
    capacity = tok_count // 4
    send_rows = experts_all * capacity
    head_count = HEADS
    head_size = model_width // head_count
    half_size = head_size // 2
    score_scale = head_size ** (-0.5)
    slot_order = deal_order[0]
    iota = jnp.arange(tok_count, dtype=jnp.int32)

    group_x = plan.gather_peers(layer_input).reshape(-1, model_width)
    group_dy = plan.gather_peers(output_grad).reshape(-1, model_width)
    group_prev = plan.gather_peers(prev_logits).reshape(-1, choice_count)
    group_slots = plan.gather_peers(deal_order).reshape(-1)
    given_rows = (plan.peer_order()[:, None] * tok_count + iota[None, :]).reshape(-1)
    deal_pick = (slot_order[:, None] == given_rows[None, :]).astype(low)
    own_rows = plan.me * tok_count + iota
    home_pick = (group_slots[None, :] == own_rows[:, None]).astype(low)

    dealt_rows = mm(deal_pick, group_x)
    dy_low = mm(deal_pick, group_dy).astype(low)
    prev_dealt = mm(deal_pick, group_prev)
    grad_out = dy_low.astype(wide)

    choices = jnp.arange(choice_count, dtype=jnp.int32)
    route_onehot = (routes[..., None] == choices).astype(wide)
    hits = jnp.sum(route_onehot, axis=1)
    earlier = mm((iota[None, :] < iota[:, None]).astype(low), hits.astype(low))
    rank = jnp.sum(route_onehot * earlier[:, None, :], axis=-1).astype(jnp.int32)
    is_ffn = routes < experts_all
    target = jnp.where(is_ffn, routes * capacity + rank, send_rows)
    places = jnp.arange(send_rows, dtype=jnp.int32)
    pick_0 = target[:, 0][:, None] == places[None, :]
    pick_1 = target[:, 1][:, None] == places[None, :]
    both_pick = (pick_0 | pick_1).astype(low)

    def to_experts(rows, extra=None):
        outgoing = mm_tn(both_pick, rows).astype(low)
        outgoing = outgoing.reshape(peer_count, local_experts * capacity, model_width)
        if extra is not None:
            outgoing = jnp.concatenate([outgoing, extra], axis=1)
        return lax.all_to_all(outgoing, "expert", split_axis=0, concat_axis=0, tiled=True)

    dy_in = to_experts(dy_low)
    dy_blocks = plan.gather_groups(dy_in)

    normed_first, unit_first, inverse_first = norm_forward(dealt_rows, attention_gain)
    first_low = normed_first.astype(low)
    projected = mm(first_low, attention_in)
    projected = projected.reshape(tok_count, 3, head_count, head_size)
    cosine_table, sine_table = rope_tables(tok_count, half_size)
    query_rot = rotate(projected[:, 0], cosine_table, sine_table, 1.0).astype(low)
    key_rot = rotate(projected[:, 1], cosine_table, sine_table, 1.0).astype(low)
    value_low = projected[:, 2].astype(low)
    allowed = (iota[None, :] <= iota[:, None]) & (iota[None, :] < lengths[0])
    raw_scores = (
        jnp.einsum("ihd,jhd->hij", query_rot, key_rot, preferred_element_type=wide) * score_scale
    )
    scores = jnp.where(allowed[None], raw_scores, -jnp.inf)
    score_peak = jnp.max(scores, axis=-1, keepdims=True)
    exp_scores = jnp.exp(scores - score_peak)
    score_probs = exp_scores / jnp.sum(exp_scores, axis=-1, keepdims=True)
    probs_low = score_probs.astype(low)
    attended = (
        jnp.einsum("hij,jhd->ihd", probs_low, value_low, preferred_element_type=wide)
        .astype(low)
        .reshape(tok_count, model_width)
    )
    residual = dealt_rows + mm(attended, attention_out)
    normed_second, unit_second, inverse_second = norm_forward(residual, mixture_gain)
    second_low = normed_second.astype(low)

    logits = mm(second_low, router_weight) + prev_dealt
    picked = jnp.sum(route_onehot * logits[:, None, :], axis=-1)
    gate_values = jax.nn.softmax(picked, axis=-1)
    gates_sent = jnp.sum(
        jnp.where(pick_0, gate_values[:, 0:1], 0.0) + jnp.where(pick_1, gate_values[:, 1:2], 0.0), axis=0
    )
    gates_sent = gates_sent.reshape(peer_count, 1, local_experts * capacity)
    gates_high = gates_sent.astype(low)
    gates_rest = (gates_sent - gates_high.astype(wide)).astype(low)
    gap = 128 - local_experts * capacity
    gates_high = jnp.pad(gates_high, ((0, 0), (0, 0), (0, gap)))
    gates_rest = jnp.pad(gates_rest, ((0, 0), (0, 0), (0, gap)))
    gate_lanes = jnp.concatenate([gates_high, gates_rest], axis=2)
    gate_lanes = jnp.pad(gate_lanes, ((0, 0), (0, 7), (0, model_width - 256)))
    x_in = to_experts(second_low, gate_lanes)
    x_blocks = plan.gather_groups(x_in)
    mix_logits = mm(second_low, constant_mix).reshape(tok_count, 2, 2)
    mix_weights = jax.nn.softmax(mix_logits, axis=-1)
    const_rows = constant_value.astype(wide).T
    const_out = (
        mix_weights[:, :, 0:1] * normed_second[:, None, :]
        + mix_weights[:, :, 1:2] * const_rows[None]
    )

    produced = expert_call(x_in, dy_in, expert_gate_up, expert_down, capacity)
    produced = lax.all_to_all(produced, "expert", split_axis=0, concat_axis=0, tiled=True)
    returned = produced[:, 0].reshape(send_rows, model_width)
    row_grads = produced[:, 1].reshape(send_rows, model_width)

    pick_0_low, pick_1_low = pick_0.astype(low), pick_1.astype(low)
    route_out = jnp.stack([mm(pick_0_low, returned), mm(pick_1_low, returned)], axis=1)
    copy_mask = routes == experts_all + 1
    const_mask = routes[..., None] == (experts_all + 2 + jnp.arange(2, dtype=jnp.int32))
    branch = (
        route_out
        + jnp.where(copy_mask[..., None], normed_second[:, None, :], 0.0)
        + jnp.where(const_mask[..., 0:1], const_out[:, 0][:, None, :], 0.0)
        + jnp.where(const_mask[..., 1:2], const_out[:, 1][:, None, :], 0.0)
    )
    output = residual + jnp.sum(gate_values[..., None] * branch, axis=1)
    group_out = plan.gather_peers(output.astype(low)).reshape(-1, model_width)
    out_rows = mm(home_pick, group_out).astype(low)

    grad_gate = jnp.sum(branch * grad_out[:, None, :], axis=-1)
    grad_picked = gate_values * (
        grad_gate - jnp.sum(gate_values * grad_gate, axis=-1, keepdims=True)
    )
    grad_logits = jnp.sum(route_onehot * grad_picked[..., None], axis=1)
    expert_input_grad = gate_values[:, 0:1] * mm(pick_0_low, row_grads) + gate_values[
        :, 1:2
    ] * mm(pick_1_low, row_grads)
    const_weight = jnp.sum(jnp.where(const_mask, gate_values[..., None], 0.0), axis=1)
    copy_weight = jnp.sum(jnp.where(copy_mask, gate_values, 0.0), axis=1)
    along_normed = jnp.sum(grad_out * normed_second, axis=-1)
    along_value = mm(dy_low, constant_value)
    grad_mix = jnp.stack(
        [const_weight * along_normed[:, None], const_weight * along_value], axis=-1
    )
    grad_mixlog = mix_weights * (grad_mix - jnp.sum(mix_weights * grad_mix, axis=-1, keepdims=True))
    grad_mixlog = grad_mixlog.reshape(tok_count, 4)
    second_wide = second_low.astype(wide)
    narrow = jnp.concatenate([grad_logits, grad_mixlog], axis=1)
    narrow_grad = jnp.dot(second_wide.T, narrow, precision=highest)
    value_grad = jnp.dot(grad_out.T, const_weight * mix_weights[:, :, 1], precision=highest)
    direct_scale = copy_weight + jnp.sum(const_weight * mix_weights[:, :, 0], axis=1)
    narrow_weight = jnp.concatenate([router_weight, constant_mix], axis=1).astype(wide)
    grad_second = (
        direct_scale[:, None] * grad_out
        + expert_input_grad
        + jnp.dot(narrow, narrow_weight.T, precision=highest)
    )
    back_second, gain_second = norm_backward(grad_second, unit_second, inverse_second, mixture_gain)
    grad_residual = grad_out + back_second

    grad_attn = grad_residual.astype(low)
    out_partial = mm_tn(attended, grad_attn)
    grad_attended = lax.dot_general(
        grad_attn, attention_out, (((1,), (1,)), ((), ())), preferred_element_type=wide
    )
    grad_attended = grad_attended.astype(low).reshape(tok_count, head_count, head_size)
    grad_value = jnp.einsum("hij,ihd->jhd", probs_low, grad_attended, preferred_element_type=wide)
    grad_probs = jnp.einsum("ihd,jhd->hij", grad_attended, value_low, preferred_element_type=wide)
    grad_scores = (
        score_probs * (grad_probs - jnp.sum(score_probs * grad_probs, axis=-1, keepdims=True))
    ).astype(low)
    grad_query = (
        jnp.einsum("hij,jhd->ihd", grad_scores, key_rot, preferred_element_type=wide) * score_scale
    )
    grad_key = (
        jnp.einsum("hij,ihd->jhd", grad_scores, query_rot, preferred_element_type=wide)
        * score_scale
    )
    grad_qkv = jnp.stack(
        [
            rotate(grad_query, cosine_table, sine_table, -1.0),
            rotate(grad_key, cosine_table, sine_table, -1.0),
            grad_value,
        ],
        axis=1,
    )
    grad_qkv = grad_qkv.reshape(tok_count, 3 * model_width).astype(low)
    in_partial = mm_tn(first_low, grad_qkv)
    grad_first = lax.dot_general(
        grad_qkv, attention_in, (((1,), (1,)), ((), ())), preferred_element_type=wide
    )
    back_first, gain_first = norm_backward(grad_first, unit_first, inverse_first, attention_gain)
    grad_dealt = grad_residual + back_first

    group_back = plan.gather_peers(grad_dealt.astype(low)).reshape(-1, model_width)
    input_rows = mm(home_pick, group_back).astype(low)
    group_logits = plan.gather_peers(grad_logits.astype(low)).reshape(-1, choice_count)
    prev_rows = mm(home_pick, group_logits).astype(low)

    share_rows = model_width // plan.dp
    matrices = jnp.concatenate([in_partial, out_partial], axis=1).reshape(plan.dp, share_rows, -1)
    narrow_all = jnp.concatenate(
        [narrow_grad, value_grad, gain_first[:, None], gain_second[:, None]], axis=1
    )
    narrow_count = narrow_all.shape[1]
    flat = narrow_all.reshape(plan.dp, 1, share_rows * narrow_count)
    flat = jnp.pad(flat, ((0, 0), (0, 7), (0, 4 * model_width - share_rows * narrow_count)))
    total = plan.sum_rows(jnp.concatenate([matrices, flat], axis=1))
    in_grad = total[:share_rows, : 3 * model_width]
    out_grad = total[:share_rows, 3 * model_width :]
    narrow_sum = total[share_rows, : share_rows * narrow_count].reshape(share_rows, narrow_count)

    share = hidden_units // plan.dp
    if plan.near:
        up_partial, down_sum = weights_call(
            x_blocks, dy_blocks, expert_gate_up, expert_down, plan.row[None], capacity
        )
    else:
        up_partial, down_sum = weights_plain(
            x_blocks, dy_blocks, expert_gate_up, expert_down, plan.row, capacity
        )
    up_partial = up_partial.reshape(local_experts, plan.dp, share_rows, 2 * share)
    swapped = plan.swap_groups(up_partial.transpose(1, 0, 2, 3))
    swapped = swapped.reshape(plan.dp, local_experts, share_rows, 2, share)
    gate_up_sum = swapped.transpose(1, 2, 3, 0, 4).reshape(local_experts, share_rows, -1)
    return (
        out_rows,
        input_rows,
        prev_rows,
        narrow_sum[:, choice_count + 6],
        narrow_sum[:, choice_count + 7],
        in_grad,
        out_grad,
        narrow_sum[:, :choice_count],
        narrow_sum[:, choice_count : choice_count + 4],
        narrow_sum[:, choice_count + 4 : choice_count + 6],
        gate_up_sum.astype(wide),
        down_sum,
    )


def solution(mesh):
    in_specs = (
        P(("dp", "expert"), None),
        P(("dp", "expert"), None),
        P(("dp", "expert"), None),
        P("dp", "expert"),
        P(("dp", "expert"), None),
        P(("dp", "expert")),
        P(),
        P(),
        P(),
        P(),
        P(),
        P(),
        P(),
        P("expert", None, None),
        P("expert", None, None),
    )
    out_specs = (
        P(("dp", "expert"), None),
        P(("dp", "expert"), None),
        P(("dp", "expert"), None),
        P("dp"),
        P("dp"),
        P("dp", None),
        P("dp", None),
        P("dp", None),
        P("dp", None),
        P("dp", None),
        P("expert", "dp", None),
        P("expert", "dp", None),
    )
    return jax.shard_map(local, mesh=mesh, in_specs=in_specs, out_specs=out_specs, check_vma=False)
```
